32 devices in a mesh: grp: 4 (over x, core), dev: 8 (over z, y).
Axes of the slice: x: 2, y: 2, z: 4, core: 2. Of those that a mesh axis runs over, the one named last changes fastest.
Arguments:
- energies: bfloat16 [4096, 32768], P(('grp', 'dev')), may hold values from -48 to 48
- triples: int32 [4096, 3], P(('grp', 'dev')), may hold values from 0 to 113, as said below
- pair_surfaces: float32 [7200, 1024], P('dev'), may hold values from -24 to 24
- pair_slot: int32 [114, 114], replicated, may hold values from 0 to 7199, as said below
- single_surfaces: float32 [120, 32], P('dev'), may hold values from -12 to 12
- modals: float32 [120, 512], P('dev'), may hold values from -1 to 1
- mode_slot: int32 [114], replicated, may hold values from 0 to 119, as said below
Outputs:
- coefficients: bfloat16 [4096, 4096], P(('grp', 'dev'))
- triple_energy: float32 [4096], P(('grp', 'dev'))
- mean_field: float32 [120, 256], P('dev')
The draws below stay inside these ranges and needn't reach their ends.
Inputs may be any that keep to these rules, and one draw needn't show every extreme that they name: The three modes of a row are distinct. Rows come in blocks of 128, one block to each device in the order of the triples' placement; all rows of a block share their first mode m, and m * (number of groups along grp) // 114 is the block's index along grp. Counting one need for each row and each of its three pairs, the rows of one block need exactly 48 surfaces from each owner along dev, the owner of pair_slot row q being q // 900. `pair_slot`: Symmetric; for two distinct modes it names the row of pair_surfaces that holds their surface, distinct pairs naming distinct rows; the diagonal is 0. `mode_slot`: distinct modes name distinct rows.
All inputs are finite; a program needn't handle non-finite values.
Results may differ from the reference program's by a relative error of at most 0.001.
Values sent between devices are 32-bit elements; how exact they have to be, the bound alone decides.
A program may use at most 128 MiB of HBM per device.

```python
import jax
import jax.numpy as jnp
from jax import lax

M = 114
G = 32
KEEP = 16
S = 16
TRI_DEV = 128
TRIPLES = 4096
MODE_DEV = 15
MODE_SLOTS = 120
PAIR_DEV = 900
PAIR_SLOTS = 7200
N_GRP = 4
N_DEV = 8


def mode_layout(key):
    mode_order = jax.random.permutation(jax.random.fold_in(key, 11), M).astype(jnp.int32)
    ranking = jnp.zeros((M,), jnp.int32).at[mode_order].set(jnp.arange(M, dtype=jnp.int32))
    return (mode_order, ranking)


def draw_mode_slot(key, part):
    mode_order, ranking = mode_layout(key)
    return ranking % N_DEV * MODE_DEV + ranking // N_DEV


def draw_pair_slot(key, part):
    mode_order, ranking = mode_layout(key)
    owner_of = ranking % N_DEV
    cell_count = M * M
    mode_ids = jnp.arange(M, dtype=jnp.int32)
    above = mode_ids[:, None] < mode_ids[None, :]
    pair_owner = (owner_of[:, None] + owner_of[None, :]) % N_DEV
    priority = jax.random.permutation(jax.random.fold_in(key, 23), cell_count).astype(jnp.int32).reshape(M, M)
    sort_keys = jnp.where(above, pair_owner * cell_count + priority, N_DEV * cell_count + priority).reshape(cell_count)
    sorted_cells = jnp.argsort(sort_keys)
    position = jnp.zeros((cell_count,), jnp.int32).at[sorted_cells].set(jnp.arange(cell_count, dtype=jnp.int32))
    flat_owner = pair_owner.reshape(cell_count)
    flat_above = above.reshape(cell_count)
    owner_ids = jnp.arange(N_DEV, dtype=jnp.int32)
    per_owner = jnp.sum(((flat_owner[:, None] == owner_ids[None, :]) & flat_above[:, None]).astype(jnp.int32), axis=0)
    starts = jnp.cumsum(per_owner) - per_owner
    slot_ids = flat_owner * PAIR_DEV + position - starts[flat_owner]
    slot_table = jnp.where(flat_above, slot_ids, 0).reshape(M, M)
    return slot_table + slot_table.T


def pick_member(member_key, classes, avoid_first, avoid_second, mode_order):
    places = jnp.arange(MODE_DEV, dtype=jnp.int32)
    rank_grid = classes[:, None] + places[None, :] * N_DEV
    members = mode_order[jnp.minimum(rank_grid, M - 1)]
    usable = (rank_grid < M) & (members != avoid_first[:, None]) & (members != avoid_second[:, None])
    scores = jax.random.randint(member_key, rank_grid.shape, 0, 1 << 20) * MODE_DEV + places[None, :]
    scores = jnp.where(usable, scores, -1)
    chosen = jnp.argmax(scores, axis=1)
    return jnp.take_along_axis(members, chosen[:, None], axis=1)[:, 0]


def draw_triples(key, part):
    mode_order, ranking = mode_layout(key)

    def one_block(block_index):
        block_key = jax.random.fold_in(jax.random.fold_in(key, 37), block_index)
        group_id = block_index // N_DEV
        lowest = (group_id * M + N_GRP - 1) // N_GRP
        beyond = ((group_id + 1) * M + N_GRP - 1) // N_GRP
        leading = lowest + jax.random.randint(jax.random.fold_in(block_key, 1), (), 0, 1 << 20) % (beyond - lowest)
        row_ids = jnp.arange(TRI_DEV, dtype=jnp.int32)
        class_second = row_ids % N_DEV
        class_third = (class_second + row_ids // N_DEV % N_DEV) % N_DEV
        lead_column = jnp.zeros((TRI_DEV,), jnp.int32) + leading
        second = pick_member(jax.random.fold_in(block_key, 2), class_second, lead_column, lead_column, mode_order)
        third_mode = pick_member(jax.random.fold_in(block_key, 3), class_third, lead_column, second, mode_order)
        return jnp.stack([lead_column, second, third_mode], axis=1).astype(jnp.int32)
    blocks = jax.vmap(one_block)(jnp.arange(N_GRP * N_DEV, dtype=jnp.int32))
    return blocks.reshape(TRIPLES, 3)


def shard_levels(key, shape, shards, smallest, high):
    factor_of, own = 1.0, jax.random.fold_in(key, 6)
    for axis_at, blocks in shards:
        steps = jnp.exp(jax.random.uniform(jax.random.fold_in(own, axis_at), (blocks,), jnp.float32, smallest / len(shards), high / len(shards)))
        factor_of = factor_of * jnp.repeat(steps, shape[axis_at] // blocks).reshape([-1 if axis == axis_at else 1 for axis in range(len(shape))])
    return factor_of


def gaussian(rng, extent, deviation, bound, shards=(), kind=jnp.bfloat16):
    array = jax.random.normal(rng, extent, jnp.float32) * deviation
    if len(shards) > 0:
        array = shard_levels(rng, extent, shards, -0.22, 0.18) * array
    return jnp.clip(array, min=-bound, max=bound).astype(kind)


def setup_inputs(seed: int = 0) -> dict:
    key_list = jax.random.split(jax.random.key(seed), 8)
    energies = gaussian(key_list[0], (TRIPLES, G * G * G), 8.0, 48.0, ((0, 32),))
    triples = draw_triples(jax.random.fold_in(key_list[7], 71), 0)
    pair_surfaces = gaussian(key_list[2], (PAIR_SLOTS, G * G), 4.0, 24.0, ((0, 8),), jnp.float32)
    pair_slot = draw_pair_slot(jax.random.fold_in(key_list[7], 71), 0)
    single_surfaces = gaussian(key_list[4], (MODE_SLOTS, G), 2.0, 12.0, ((0, 8),), jnp.float32)
    modals = gaussian(key_list[5], (MODE_SLOTS, G * S), G ** -0.5, 1.0, ((0, 8),), jnp.float32)
    mode_slot = draw_mode_slot(jax.random.fold_in(key_list[7], 71), 0)
    return dict(energies=energies, triples=triples, pair_surfaces=pair_surfaces, pair_slot=pair_slot, single_surfaces=single_surfaces, modals=modals, mode_slot=mode_slot)


highest = lax.Precision.HIGHEST


def tables():
    orders = jnp.arange(KEEP, dtype=jnp.float32)
    points = jnp.arange(G, dtype=jnp.float32) + 0.5
    cosines = jnp.cos(jnp.pi * orders[:, None] * points[None, :] / G)
    weights = jnp.where(orders == 0, 1.0, 2.0) / G
    return cosines, weights[:, None] * cosines


def chebyshev_fit(values, fitter):
    number = values.shape[0]
    section_one = jnp.einsum('cg,bgx->bcx', fitter, values.reshape(number, G, G * G), precision=highest)
    section_one = section_one.reshape(number, KEEP, G, G)
    section_two = jnp.einsum('dh,bchl->bcdl', fitter, section_one, precision=highest)
    return jnp.einsum('el,bcdl->bcde', fitter, section_two, precision=highest)


def oriented(picked, lower_ends, upper_ends, width):
    square = picked.reshape(-1, width, width)
    return jnp.where((lower_ends < upper_ends)[:, None, None], square, jnp.swapaxes(square, 1, 2))


def reference(energies, triples, pair_surfaces, pair_slot, single_surfaces, modals, mode_slot):
    cosines, fitter = tables()
    shaped = modals.reshape(MODE_SLOTS, G, S)
    ground = jnp.einsum('mg,cg->mc', shaped[:, :, 0] ** 2, cosines, precision=highest)
    blocks = TRIPLES // TRI_DEV
    slot_range = jnp.arange(MODE_SLOTS, dtype=jnp.int32)

    def advance(totals, inputs):
        energy, mode_rows = inputs
        lead_mode = mode_rows[:, 0]
        second = mode_rows[:, 1]
        third_mode = mode_rows[:, 2]
        pair_first = oriented(pair_surfaces[pair_slot[lead_mode, second]], lead_mode, second, G)
        pair_second = oriented(pair_surfaces[pair_slot[lead_mode, third_mode]], lead_mode, third_mode, G)
        pair_third = oriented(pair_surfaces[pair_slot[second, third_mode]], second, third_mode, G)
        slot_first = mode_slot[lead_mode]
        slot_second = mode_slot[second]
        slot_third = mode_slot[third_mode]
        single_first = single_surfaces[slot_first]
        single_second = single_surfaces[slot_second]
        single_third = single_surfaces[slot_third]
        values = (energy.astype(jnp.float32).reshape(-1, G, G, G)
                  - pair_first[:, :, :, None] - pair_second[:, :, None, :] - pair_third[:, None, :, :]
                  - single_first[:, :, None, None] - single_second[:, None, :, None] - single_third[:, None, None, :])
        fitted = chebyshev_fit(values, fitter)
        ground_first = ground[slot_first]
        ground_second = ground[slot_second]
        ground_third = ground[slot_third]
        field_first = jnp.einsum('bcde,bd,be->bc', fitted, ground_second, ground_third, precision=highest)
        field_second = jnp.einsum('bcde,bc,be->bd', fitted, ground_first, ground_third, precision=highest)
        field_third = jnp.einsum('bcde,bc,bd->be', fitted, ground_first, ground_second, precision=highest)
        energy_out = jnp.sum(field_first * ground_first, axis=1)
        slot_ids = jnp.concatenate([slot_first, slot_second, slot_third])
        onehot = (slot_range[:, None] == slot_ids[None, :]).astype(jnp.float32)
        fields = jnp.concatenate([field_first, field_second, field_third], axis=0)
        totals = totals + jnp.dot(onehot, fields, precision=highest)
        return totals, (fitted.reshape(-1, KEEP * KEEP * KEEP).astype(jnp.bfloat16), energy_out)

    moments, (coefficients, triple_energy) = lax.scan(
        advance, jnp.zeros((MODE_SLOTS, KEEP), jnp.float32),
        (energies.reshape(blocks, TRI_DEV, G * G * G), triples.reshape(blocks, TRI_DEV, 3)))
    weighted = jnp.dot(moments, cosines, precision=highest)
    mean_field = jnp.einsum('mga,mg,mgb->mab', shaped, weighted, shaped, precision=highest).reshape(MODE_SLOTS, S * S)
    return coefficients.reshape(TRIPLES, KEEP * KEEP * KEEP), triple_energy.reshape(TRIPLES), mean_field
```

```python
import jax
import jax.numpy as jnp
import numpy as np
from jax import lax
from jax.experimental import pallas as pl
from jax.experimental.pallas import tpu as pltpu
from jax.sharding import PartitionSpec as P

G = 32
KEEP = 16
S = 16
PAIRS = 4

highest = lax.Precision.HIGHEST


def np_tables():
    orders = np.arange(KEEP, dtype=np.float64)
    points = np.arange(G, dtype=np.float64) + 0.5
    cosines = np.cos(np.pi * orders[:, None] * points[None, :] / G)
    weights = np.where(orders == 0, 1.0, 2.0) / G
    return cosines, weights[:, None] * cosines


COS, FIT = np_tables()
ROWSUM = FIT.astype(np.float32).sum(axis=1, dtype=np.float64)


def split(values):
    values = np.asarray(values, np.float32)
    high = values.astype(jnp.bfloat16)
    return high, (values - high.astype(np.float32)).astype(jnp.bfloat16)


PLAIN = np.einsum("dh,el->hlde", FIT, FIT).reshape(G * G, KEEP * KEEP)
SWAPPED = np.einsum("eh,dl->hlde", FIT, FIT).reshape(G * G, KEEP * KEEP)
eye = np.eye(KEEP)
SPREAD_D = np.einsum("xd,e->xde", eye, np.ones(KEEP)).reshape(KEEP, -1)
SPREAD_E = np.einsum("xe,d->xde", eye, np.ones(KEEP)).reshape(KEEP, -1)
FIRST = np.einsum("xd,e->xde", eye, ROWSUM).reshape(KEEP, -1)
SECOND = np.einsum("xe,d->xde", eye, ROWSUM).reshape(KEEP, -1)
GROUND = np.einsum("cg,s->gsc", COS, np.arange(S) == 0).reshape(G * S, KEEP)


def dot(a, b, precision=None):
    return jnp.dot(a, b, precision=precision, preferred_element_type=jnp.float32)


def pair_kernel(surf_ref, high_ref, low_ref, out_ref):
    values = surf_ref[...]
    top = values.astype(jnp.bfloat16)
    rest = (values - top.astype(jnp.float32)).astype(jnp.bfloat16)
    fitted = dot(top, high_ref[...]) + dot(top, low_ref[...]) + dot(rest, high_ref[...])
    out_ref[0] = fitted[:, : KEEP * KEEP]
    out_ref[1] = fitted[:, KEEP * KEEP :]


def pair_table(pair_surfaces):
    rows = pair_surfaces.shape[0]
    block = min(304, rows)
    steps = -(-rows // block)
    padded = steps * block
    high, low = split(np.concatenate([PLAIN, SWAPPED], axis=1))
    whole = lambda a: pl.BlockSpec(a.shape, lambda i: (0, 0))
    table = pl.pallas_call(
        pair_kernel,
        grid=(steps,),
        in_specs=[pl.BlockSpec((block, G * G), lambda i: (i, 0)), whole(high), whole(low)],
        out_specs=pl.BlockSpec((2, block, KEEP * KEEP), lambda i: (0, i, 0)),
        out_shape=jax.ShapeDtypeStruct((2, padded, KEEP * KEEP), jnp.float32),
        cost_estimate=pl.CostEstimate(
            flops=12 * rows * G * G * KEEP * KEEP, bytes_accessed=4 * rows * G * G, transcendentals=0
        ),
    )(pair_surfaces, jnp.asarray(high), jnp.asarray(low))
    return table.reshape(2 * padded, KEEP * KEEP), padded


def fit_kernel(scale_ref, front_ref, back_ref, high_ref, low_ref, acc):
    step = pl.program_id(0)
    number = front_ref.shape[0]
    high, low = high_ref[...], low_ref[...]

    @pl.when(step == 0)
    def _():
        acc[...] = jnp.zeros_like(acc)

    sums, differences = [], []
    for j in range(PAIRS):
        k = PAIRS - 1 - j
        both = jnp.concatenate(
            [front_ref[:, j * G * G : (j + 1) * G * G], back_ref[:, k * G * G : (k + 1) * G * G]],
            axis=0,
        )
        planes = dot(both, high) + dot(both, low)
        sums.append(planes[:number] + planes[number:])
        differences.append(planes[:number] - planes[number:])
    for c in range(KEEP):
        parts = sums if c % 2 == 0 else differences
        total = acc[c]
        for j in range(PAIRS):
            total += scale_ref[c, step * PAIRS + j] * parts[j]
        acc[c] = total


def field_kernel(
    acc, pair_ref, column_ref, row_ref, table_ref,
    spread_d_ref, spread_e_ref, first_ref, second_ref, expand_ref,
    coef_ref, energy_ref, partial_ref,
):
    number = acc.shape[1]
    area = KEEP * KEEP
    slots = table_ref.shape[0]
    hits = (column_ref[...] == lax.broadcasted_iota(jnp.int32, (3 * number, slots), 1))
    taken = dot(hits.astype(jnp.float32), table_ref[...], highest)
    ground, single = taken[:, :KEEP], taken[:, KEEP:]
    g1, g2, g3 = (ground[i * number : (i + 1) * number] for i in range(3))
    s1, s2, s3 = (single[i * number : (i + 1) * number] for i in range(3))
    g2e = dot(g2, spread_d_ref[...], highest)
    g3e = dot(g3, spread_e_ref[...], highest)
    weight = g2e * g3e
    p12 = pair_ref[:number] + dot(s1, first_ref[...], highest) + dot(s2, second_ref[...], highest)
    p13 = pair_ref[number : 2 * number] + dot(s3, second_ref[...], highest)
    p23 = pair_ref[2 * number :]

    def halves(values):
        top = values.astype(jnp.bfloat16).astype(jnp.float32)
        return top, values - top

    pieces = halves(p12) + halves(p13)
    lane = lax.broadcasted_iota(jnp.int32, (number, KEEP), 1)
    f1 = jnp.zeros((number, KEEP), jnp.float32)
    mixed = jnp.zeros((number, area), jnp.float32)
    for c in range(KEEP):
        left = jnp.concatenate([p[:, c * KEEP : (c + 1) * KEEP] for p in pieces], axis=1)
        correction = dot(left.astype(jnp.bfloat16), expand_ref[...])
        fitted = acc[c] - correction - p23 * float(ROWSUM[c])
        coef_ref[:, c * area : (c + 1) * area] = fitted.astype(jnp.bfloat16)
        f1 = f1 + jnp.where(lane == c, jnp.sum(fitted * weight, axis=1, keepdims=True), 0.0)
        mixed = mixed + g1[:, c : c + 1] * fitted
    gather = lambda a, b: lax.dot_general(
        a, b, (((1,), (1,)), ((), ())), precision=highest, preferred_element_type=jnp.float32
    )
    f2 = gather(mixed * g3e, spread_d_ref[...])
    f3 = gather(mixed * g2e, spread_e_ref[...])
    energy_ref[...] = jnp.sum(f1 * g1, axis=1, keepdims=True)
    fields = jnp.concatenate([f1, f2, f3], axis=0)
    hits_t = (row_ref[...] == lax.broadcasted_iota(jnp.int32, (slots, 3 * number), 0))
    partial_ref[...] = dot(hits_t.astype(jnp.float32), fields, highest)


def fit(energies):
    number = energies.shape[0]
    steps = G // 2 // PAIRS
    blocks = G // PAIRS
    high, low = split(PLAIN)
    whole = lambda a: pl.BlockSpec(a.shape, lambda i: (0, 0))
    width = PAIRS * G * G
    area = KEEP * KEEP
    return pl.pallas_call(
        fit_kernel,
        grid=(steps,),
        in_specs=[
            pl.BlockSpec(memory_space=pltpu.SMEM),
            pl.BlockSpec((number, width), lambda i: (0, i)),
            pl.BlockSpec((number, width), lambda i: (0, blocks - 1 - i)),
            whole(high),
            whole(low),
        ],
        out_specs=pl.BlockSpec((KEEP, number, area), lambda i: (0, 0, 0)),
        out_shape=jax.ShapeDtypeStruct((KEEP, number, area), jnp.float32),
        cost_estimate=pl.CostEstimate(
            flops=4 * number * G * G * G * area, bytes_accessed=2 * number * G * G * G, transcendentals=0
        ),
        compiler_params=pltpu.CompilerParams(dimension_semantics=("arbitrary",)),
    )(jnp.asarray(FIT.astype(np.float32)), energies, energies, jnp.asarray(high), jnp.asarray(low))


def fields(fitted, pair_terms, slot_ids, table):
    number = fitted.shape[1]
    first, second = FIRST.astype(np.float32), SECOND.astype(np.float32)
    spread_d, spread_e = SPREAD_D.astype(np.float32), SPREAD_E.astype(np.float32)
    expand = np.concatenate([first, first, second, second], axis=0).astype(jnp.bfloat16)
    return pl.pallas_call(
        field_kernel,
        out_shape=[
            jax.ShapeDtypeStruct((number, KEEP * KEEP * KEEP), jnp.bfloat16),
            jax.ShapeDtypeStruct((number, 1), jnp.float32),
            jax.ShapeDtypeStruct((table.shape[0], KEEP), jnp.float32),
        ],
    )(
        fitted, pair_terms, slot_ids[:, None], slot_ids[None, :], table,
        jnp.asarray(spread_d), jnp.asarray(spread_e), jnp.asarray(first), jnp.asarray(second),
        jnp.asarray(expand),
    )


def body(energies, triples, pair_surfaces, pair_slot, single_surfaces, modals, mode_slot):
    devices = lax.axis_size("dev")
    groups = lax.axis_size("grp")
    number = triples.shape[0]
    pair_rows = pair_surfaces.shape[0]
    mode_rows = modals.shape[0]
    modes = mode_slot.shape[0]
    capacity = 3 * number // devices
    cosines = jnp.asarray(COS.astype(np.float32))
    fitter = jnp.asarray(FIT.astype(np.float32))

    pairs, padded = pair_table(pair_surfaces)

    local_ground = jnp.dot(modals * modals, jnp.asarray(GROUND.astype(np.float32)), precision=highest)
    local_single = jnp.dot(single_surfaces, fitter.T, precision=highest)
    local_modes = jnp.concatenate([local_ground, local_single], axis=1).reshape(1, -1)

    a1, a2, a3 = triples[:, 0], triples[:, 1], triples[:, 2]
    lower = jnp.concatenate([a1, a1, a2])
    upper = jnp.concatenate([a2, a3, a3])
    mode_ids = jnp.arange(modes, dtype=jnp.int32)
    lines = jnp.dot(
        (lower[:, None] == mode_ids[None, :]).astype(jnp.float32),
        pair_slot.astype(jnp.float32),
        precision=highest,
    )
    pair_ids = jnp.sum(jnp.where(upper[:, None] == mode_ids[None, :], lines, 0.0), axis=1)
    pair_ids = (pair_ids + 0.5).astype(jnp.int32)
    all_modes = jnp.concatenate([a1, a2, a3])
    slot_ids = jnp.sum(
        jnp.where(all_modes[:, None] == mode_ids[None, :], mode_slot[None, :], 0), axis=1
    )
    owners = pair_ids // pair_rows
    local_rows = pair_ids - owners * pair_rows + jnp.where(lower < upper, 0, padded)
    index = jnp.arange(3 * number, dtype=jnp.int32)
    earlier = (owners[:, None] == owners[None, :]) & (index[:, None] < index[None, :])
    places = owners * capacity + jnp.sum(earlier.astype(jnp.int32), axis=0)
    requests = jnp.sum(jnp.where(places[:, None] == index[None, :], local_rows[:, None], 0), axis=0)

    sent = jnp.concatenate(
        [
            requests.astype(jnp.float32).reshape(devices, capacity),
            jnp.broadcast_to(local_modes, (devices, local_modes.shape[1])),
        ],
        axis=1,
    )
    received = lax.all_to_all(sent, "dev", split_axis=0, concat_axis=0, tiled=True)
    wanted = received[:, :capacity].astype(jnp.int32).reshape(-1)
    table = received[:, capacity:].reshape(devices * mode_rows, 2 * KEEP)
    answers = pairs[wanted].reshape(devices, capacity, KEEP * KEEP)
    arrived = lax.all_to_all(answers, "dev", split_axis=0, concat_axis=0, tiled=True)
    pair_terms = arrived.reshape(devices * capacity, KEEP * KEEP)[places]

    coefficients, energy, partial = fields(fit(energies), pair_terms, slot_ids, table)

    spread = jnp.broadcast_to(
        partial.reshape(1, devices, mode_rows, KEEP), (groups, devices, mode_rows, KEEP)
    ).reshape(groups * devices, mode_rows, KEEP)
    moments = jnp.sum(
        lax.all_to_all(spread, ("grp", "dev"), split_axis=0, concat_axis=0, tiled=True), axis=0
    )
    weighted = jnp.dot(moments, cosines, precision=highest)
    shaped = modals.reshape(mode_rows, G, S)
    mean_field = jnp.einsum("mga,mg,mgb->mab", shaped, weighted, shaped, precision=highest)
    return coefficients, energy.reshape(number), mean_field.reshape(mode_rows, S * S)


def solution(mesh):
    in_specs = (
        P(("grp", "dev"), None),
        P(("grp", "dev"), None),
        P("dev", None),
        P(),
        P("dev", None),
        P("dev", None),
        P(),
    )
    out_specs = (P(("grp", "dev"), None), P(("grp", "dev")), P("dev", None))
    return jax.shard_map(body, mesh=mesh, in_specs=in_specs, out_specs=out_specs, check_vma=False)
```
